32 devices in a mesh: dp: 2 (over y), seq: 4 (over z), weight: 4 (over x, core).
Axes of the slice: x: 2, y: 2, z: 4, core: 2. Of those that a mesh axis runs over, the one named last changes fastest.
Arguments:
- tokens: bfloat16 [96, 200, 512], P(('dp', 'seq', 'weight')), may hold values from -6 to 6
- valid: int32 [96, 200], P(('dp', 'seq', 'weight')), may hold values from 0 to 1, as said below
- experts: int32 [96, 200, 2], P(('dp', 'seq', 'weight')), may hold values from 0 to 31, as said below
- slots: int32 [96, 200, 2], P(('dp', 'seq', 'weight')), may hold values from 0 to 47, as said below
- ln1_gain: float32 [512], replicated, may hold values from 0.5 to 1.5
- ln1_bias: float32 [512], replicated, may hold values from -3 to 3
- w_qkv: bfloat16 [512, 1536], replicated, may hold values from -0.875 to 0.875
- w_out: bfloat16 [512, 512], replicated, may hold values from -2.5 to 2.5
- ln2_gain: float32 [512], replicated, may hold values from 0.5 to 1.5
- ln2_bias: float32 [512], replicated, may hold values from -3 to 3
- w_router: bfloat16 [512, 32], replicated, may hold values from -0.5 to 0.5
- w_in: bfloat16 [32, 512, 2048], P(None, None, 'weight'), may hold values from -0.25 to 0.25
- w_back: bfloat16 [32, 2048, 512], P(None, 'weight'), may hold values from -6 to 6
- cotangent: bfloat16 [96, 200, 512], P(('dp', 'seq', 'weight')), may hold values from -6 to 6
Outputs:
- output: bfloat16 [96, 200, 512], P(('dp', 'seq', 'weight'))
- grad_tokens: bfloat16 [96, 200, 512], P(('dp', 'seq', 'weight'))
- grad_ln1_gain: float32 [512], replicated
- grad_ln1_bias: float32 [512], replicated
- grad_qkv: float32 [512, 1536], replicated
- grad_out: float32 [512, 512], replicated
- grad_ln2_gain: float32 [512], replicated
- grad_ln2_bias: float32 [512], replicated
- grad_router: float32 [512, 32], replicated
- grad_in: float32 [32, 512, 2048], P(('dp', 'seq'), None, 'weight')
- grad_back: float32 [32, 2048, 512], P(('dp', 'seq'), 'weight')
- rms: float32 [3], replicated
The draws below stay inside these ranges and needn't reach their ends.
Inputs may be any that keep to these rules, and one draw needn't show every extreme that they name: Each token, padding positions too, names 2 different experts. `valid`: exactly 3 positions of each image are 0. Within one device's tokens, taken image by image, position by position, and k = 0 before k = 1, slots[t, k] counts the earlier pairs of valid tokens that name the same expert, and is 47 where that count reaches 47; pairs of padding positions have 47. Every device has an expert that is named more than 47 times.
All inputs are finite; a program needn't handle non-finite values.
Results may differ from the reference program's by a relative error of at most 0.015.
Values may be sent and summed in bfloat16 or wider, within the bound.
No kernel may reach another device: no remote copies, remote signals or barrier semaphores. Data moves between devices by JAX's collectives and lax.ppermute only.
A program may use at most 320 MiB of HBM per device.

```python
from functools import partial
import jax
import jax.numpy as jnp
from jax import lax

HEADS = 8
HEAD_DIM = 64
D = 512
FF = 2048
EXPERTS = 32
TOP = 2
PAD_LEN = 200
VALID = 197
IMG_G = 12
IMAGES = 96
TOK_DEV = 600
CAP = 47
N_DP = 2
N_SEQ = 4
N_WEIGHT = 4


def valid_table(key):
    base_key = jax.random.fold_in(key, 3)
    ranking = jax.random.randint(base_key, (IMAGES, PAD_LEN), 0, 4096) * PAD_LEN + jnp.arange(PAD_LEN, dtype=jnp.int32)
    places = jnp.argsort(jnp.argsort(ranking, axis=1), axis=1)
    return (places >= PAD_LEN - VALID).astype(jnp.int32)


def route_tables(key):
    base_key = jax.random.fold_in(key, 7)
    first_key, second_key, third_key, fourth_key, fifth_key = jax.random.split(base_key, 5)
    block_count = N_DP * N_SEQ * N_WEIGHT
    valid_rows = valid_table(key).reshape(block_count, TOK_DEV)
    first_pick = jax.random.randint(first_key, (block_count, TOK_DEV), 0, EXPERTS)
    step_pick = jax.random.randint(second_key, (block_count, TOK_DEV), 1, EXPERTS)
    hot_expert = jax.random.randint(third_key, (block_count, 1), 0, EXPERTS)
    hot_count = jnp.minimum(CAP + jax.random.randint(fourth_key, (block_count, 1), 1, CAP // 2 + 2), TOK_DEV // 2)
    ranking = jax.random.randint(fifth_key, (block_count, TOK_DEV), 0, 4096) * TOK_DEV
    ranking = ranking + jnp.arange(TOK_DEV, dtype=jnp.int32) + (1 - valid_rows) * (4096 * TOK_DEV)
    places = jnp.argsort(jnp.argsort(ranking, axis=1), axis=1)
    first_pick = jnp.where(places < hot_count, hot_expert, first_pick)
    second_pick = (first_pick + step_pick) % EXPERTS
    pair_ids = jnp.stack([first_pick, second_pick], axis=-1).reshape(block_count, TOK_DEV * TOP)
    live_pairs = jnp.repeat(valid_rows, TOP, axis=1)
    one_hot = ((pair_ids[..., None] == jnp.arange(EXPERTS, dtype=jnp.int32)) & (live_pairs[..., None] > 0)).astype(jnp.int32)
    earlier = jnp.cumsum(one_hot, axis=1) - one_hot
    pair_rank = jnp.sum(earlier * one_hot, axis=-1)
    slot_ids = jnp.where(live_pairs > 0, jnp.minimum(pair_rank, CAP), CAP)
    expert_ids = pair_ids.reshape(IMAGES, PAD_LEN, TOP)
    slot_ids = slot_ids.reshape(IMAGES, PAD_LEN, TOP)
    return (expert_ids.astype(jnp.int32), slot_ids.astype(jnp.int32))


def draw_valid(key, part):
    return valid_table(key)


def draw_experts(key, part):
    return route_tables(key)[0]


def draw_slots(key, part):
    return route_tables(key)[1]


def levels(key, dims, cuts, least, largest):
    def one(dim, blocks):
        heights = jax.random.uniform(jax.random.fold_in(jax.random.fold_in(key, 6), dim), (blocks,), jnp.float32, least / len(cuts), largest / len(cuts))
        return jnp.repeat(jnp.exp(heights), dims[dim] // blocks).reshape((-1,) + (1,) * (len(dims) - dim - 1))

    gain = one(*cuts[0])
    for cut in cuts[1:]:
        gain = gain * one(*cut)
    return gain


def scatter_about(stream_key, dims, width, bound, pieces=(), kind=jnp.bfloat16):
    gain = levels(stream_key, dims, pieces, -0.22, 0.18) if pieces else 1.0
    entries = jax.random.normal(stream_key, dims, jnp.float32) * width * gain
    return jnp.minimum(jnp.maximum(entries, -bound), bound).astype(kind)


def setup_inputs(seed: int = 0) -> dict:
    key_of = jax.random.split(jax.random.key(seed), 15)
    tokens = scatter_about(key_of[0], (IMAGES, PAD_LEN, D), 1.0, 6.0, ((0, 32),))
    valid = draw_valid(jax.random.fold_in(key_of[14], 71), 0)
    experts = draw_experts(jax.random.fold_in(key_of[14], 71), 0)
    slots = draw_slots(jax.random.fold_in(key_of[14], 71), 0)
    ln1_gain = jnp.clip(1.0 + 0.1 * jax.random.normal(key_of[4], (D,), jnp.float32), 0.5, 1.5)
    ln1_bias = scatter_about(key_of[5], (D,), 0.3, 3.0, (), jnp.float32)
    w_qkv = scatter_about(key_of[6], (D, 3 * D), (1.36 * D ** -0.5), 0.875)
    w_out = scatter_about(key_of[7], (D, D), (4.0 * D ** -0.5), 2.5)
    ln2_gain = jnp.clip(1.0 + 0.1 * jax.random.normal(key_of[8], (D,), jnp.float32), 0.5, 1.5)
    ln2_bias = scatter_about(key_of[9], (D,), 0.3, 3.0, (), jnp.float32)
    w_router = scatter_about(key_of[10], (D, EXPERTS), (0.75 * D ** -0.5), 0.5)
    w_in = scatter_about(key_of[11], (EXPERTS, D, FF), D ** -0.5, 0.25, ((2, 4),))
    w_back = scatter_about(key_of[12], (EXPERTS, FF, D), (22.0 * FF ** -0.5), 6.0, ((1, 4),))
    cotangent = scatter_about(key_of[13], (IMAGES, PAD_LEN, D), 1.0, 6.0, ((0, 32),))
    return dict(tokens=tokens, valid=valid, experts=experts, slots=slots, ln1_gain=ln1_gain, ln1_bias=ln1_bias, w_qkv=w_qkv, w_out=w_out, ln2_gain=ln2_gain, ln2_bias=ln2_bias, w_router=w_router, w_in=w_in, w_back=w_back, cotangent=cotangent)


@jax.custom_vjp
def low(v):
    return lax.optimization_barrier(v.astype(jnp.bfloat16)).astype(jnp.float32)

@jax.custom_vjp
def low_back(v):
    return v

def low_keep(v):
    return (low(v), None)

def low_pass(kept, grad):
    return (grad,)

def back_keep(v):
    return (v, None)

def back_low(kept, grad):
    return (low(grad),)
low.defvjp(low_keep, low_pass)
low_back.defvjp(back_keep, back_low)

def layer_norm(values, gain_row, shift_row):
    centre = lax.optimization_barrier(jnp.mean(values, axis=-1, keepdims=True))
    offset = values - centre
    spread = lax.optimization_barrier(jnp.mean(offset * offset, axis=-1, keepdims=True))
    return offset * lax.rsqrt(spread + 1e-06) * gain_row + shift_row

def to_blocks(blocked):
    trailing = blocked.shape[2:]
    return blocked.reshape((N_DP * N_SEQ, N_WEIGHT, TOK_DEV) + trailing)

def from_blocks(blocked):
    trailing = blocked.shape[3:]
    return blocked.reshape((IMAGES, PAD_LEN) + trailing)

def attend(block_data):
    qkv_block, valid_block = block_data
    query_rows = qkv_block[:, :, 0]
    key_rows = qkv_block[:, :, 1]
    value_rows = qkv_block[:, :, 2]
    raw_scores = jnp.einsum('iqhd,ikhd->ihqk', query_rows, key_rows, precision=lax.Precision.HIGHEST) * HEAD_DIM ** (-0.5)
    scores = jnp.where(valid_block[:, None, None, :] > 0, low_back(raw_scores), -1e+30)
    weights = jax.nn.softmax(scores, axis=-1)
    return jnp.einsum('ihqk,ikhd->iqhd', low(weights), value_rows, precision=lax.Precision.HIGHEST)

def scatter_pairs(token_rows, flat_index):
    slot_table = jnp.zeros((CAP * EXPERTS + 1, D), jnp.float32)
    slot_table = slot_table.at[flat_index.reshape(-1)].add(jnp.repeat(token_rows, TOP, axis=0))
    return slot_table[:CAP * EXPERTS]

def pick_pairs(slot_table, flat_index):
    return jnp.take(slot_table, flat_index, axis=0)

def forward(valid, experts, slots, tokens, ln1_gain, ln1_bias, w_qkv, w_out, ln2_gain, ln2_bias, w_router, w_in, w_back):
    highest = lax.Precision.HIGHEST
    valid_rows = valid.astype(jnp.float32)[..., None]
    normed = low(layer_norm(tokens, ln1_gain, ln1_bias) * valid_rows)
    qkv_rows = low_back(low(jnp.dot(normed.reshape(-1, D), w_qkv, precision=highest)))
    qkv_rows = qkv_rows.reshape(N_DP * N_WEIGHT, IMG_G, PAD_LEN, 3, HEADS, HEAD_DIM)
    context = lax.map(jax.checkpoint(attend), (qkv_rows, valid.reshape(N_DP * N_WEIGHT, IMG_G, PAD_LEN)))
    context = low_back(low(context.reshape(-1, D)))
    branch = low_back(jnp.dot(context, w_out, precision=highest)).reshape(IMAGES, PAD_LEN, D) * valid_rows
    middle = tokens + branch
    routed = low(layer_norm(middle, ln2_gain, ln2_bias) * valid_rows)
    logits = jnp.dot(routed.reshape(-1, D), w_router, precision=highest)
    router_probs = jax.nn.softmax(logits, axis=-1).reshape(IMAGES, PAD_LEN, 1, EXPERTS)
    chosen = (experts[..., None] == jnp.arange(EXPERTS, dtype=jnp.int32)).astype(jnp.float32)
    gate_values = lax.optimization_barrier(jnp.sum(router_probs * chosen, axis=-1))
    flat_index = jnp.where(slots < CAP, slots * EXPERTS + experts, CAP * EXPERTS).astype(jnp.int32)
    flat_blocks = to_blocks(flat_index)
    buffers = jax.vmap(jax.vmap(scatter_pairs))(to_blocks(routed), flat_blocks)
    buffers = buffers.reshape(N_DP * N_SEQ, N_WEIGHT * CAP, EXPERTS, D)

    def expert_block(block_rows):
        pre_act = low_back(jnp.einsum('ced,edf->cef', block_rows, w_in, precision=highest))
        hidden = low(jax.nn.gelu(pre_act))
        return low_back(jnp.einsum('cef,efd->ced', hidden, w_back, precision=highest))
    returned = lax.map(jax.checkpoint(expert_block), buffers)
    returned = returned.reshape(N_DP * N_SEQ, N_WEIGHT, CAP * EXPERTS, D)
    returned = jnp.concatenate([returned, jnp.zeros((N_DP * N_SEQ, N_WEIGHT, 1, D), jnp.float32)], axis=2)
    picked = from_blocks(jax.vmap(jax.vmap(pick_pairs))(returned, flat_blocks))
    mixture = lax.optimization_barrier(jnp.sum(gate_values[..., None] * picked, axis=2))
    final_rows = middle + mixture
    return (final_rows, (branch, mixture, final_rows * valid_rows))

def reference(tokens, valid, experts, slots, ln1_gain, ln1_bias, w_qkv, w_out, ln2_gain, ln2_bias, w_router, w_in, w_back, cotangent):
    inputs = (tokens, ln1_gain, ln1_bias, w_qkv, w_out, ln2_gain, ln2_bias, w_router, w_in, w_back)
    floats = tuple((member.astype(jnp.float32) for member in inputs))
    final_rows, pullback, extras = jax.vjp(partial(forward, valid, experts, slots), *floats, has_aux=True)
    gradients = pullback(cotangent.astype(jnp.float32))
    square_sums = jnp.stack([jnp.sum(member * member) for member in extras])
    rms_values = jnp.sqrt(square_sums / (IMAGES * VALID * D))
    return (final_rows.astype(jnp.bfloat16), gradients[0].astype(jnp.bfloat16), gradients[1], gradients[2], gradients[3], gradients[4], gradients[5], gradients[6], gradients[7], gradients[8], gradients[9], rms_values)
```

```python
import functools

import jax
import jax.numpy as jnp
from jax import lax
from jax.experimental import pallas as pl
from jax.experimental.pallas import tpu as pltpu
from jax.sharding import PartitionSpec as P

HEADS = 8
HEAD_DIM = 64
TOP = 2
VALID = 197
CAP = 47
ROWS = 48
EVERY = ("dp", "seq", "weight")
GROUP = ("dp", "seq")
PLANE = ("dp", "weight")
PAIR = 2 * HEAD_DIM
SCALE = HEAD_DIM ** (-0.5)
BF = jnp.bfloat16
F32 = jnp.float32
CURVE = 0.7978845608028654
CUBIC = 0.044715
VMEM = 60 * 1024 * 1024


def iota(shape, dim):
    return lax.broadcasted_iota(jnp.int32, shape, dim)


def mm(a, b, dims=((1,), (0,)), precision=None):
    return lax.dot_general(a, b, (dims, ((), ())), precision=precision, preferred_element_type=F32)


def mm_exact(a, b):
    return mm(a, b, precision=lax.Precision.HIGHEST)


def parts3(v):
    high = v.astype(BF)
    rest = v - high.astype(F32)
    mid = rest.astype(BF)
    low = (rest - mid.astype(F32)).astype(BF)
    return high, mid, low


def ln_stats(v):
    centre = jnp.mean(v, axis=-1, keepdims=True)
    off = v - centre
    spread = jnp.mean(off * off, axis=-1, keepdims=True)
    r = lax.rsqrt(spread + 1e-06)
    return off * r, r


def ln_back(u, n, r, gain):
    ug = u * gain
    return r * (
        ug - jnp.mean(ug, axis=-1, keepdims=True) - n * jnp.mean(ug * n, axis=-1, keepdims=True)
    )


def one_hot_rows(index_ref, first_row, row_count):
    width = index_ref.shape[-1]
    rows = iota((row_count, width), 0) + first_row
    hit = (rows == index_ref[0:1, :]) | (rows == index_ref[1:2, :])
    return jnp.where(hit, 1.0, 0.0).astype(BF)


def one_hot_tokens(index, row_count):
    rows = iota((index.shape[0], row_count), 1)
    hit = (rows == index[:, 0:1]) | (rows == index[:, 1:2])
    return jnp.where(hit, 1.0, 0.0).astype(BF)


def head_masks():
    lane = iota((1, PAIR), 1)
    first = jnp.where(lane < HEAD_DIM, 1.0, 0.0)
    return first.astype(BF), (1.0 - first).astype(BF)


def send_kernel(index_ref, rows_ref, out_ref, flat_ref, *, images, length, chunk):
    flat_ref[...] = jnp.zeros(flat_ref.shape, F32)
    for i in range(images):
        flat_ref[i * length : (i + 1) * length, :] = rows_ref[i].astype(F32)
    scatter_rows(index_ref, flat_ref, out_ref, chunk)


def scatter_rows(index_ref, flat_ref, out_ref, chunk):
    flat = flat_ref[...].astype(BF)
    blocks = out_ref.shape[0]
    width = out_ref.shape[2]

    def body(j, carry):
        hot = one_hot_rows(index_ref, j * (chunk * ROWS), chunk * ROWS)
        out = mm(hot, flat).astype(BF)
        out_ref[pl.ds(j * chunk, chunk)] = out.reshape(chunk, ROWS, width)
        return carry

    lax.fori_loop(0, blocks // chunk, body, 0)


def forward_kernel(
    x_ref,
    col_ref,
    row_ref,
    index_ref,
    gain1_ref,
    bias1_ref,
    w_qkv_ref,
    w_out_ref,
    gain2_ref,
    bias2_ref,
    w_router_ref,
    qkv_ref,
    ctx_ref,
    mid_ref,
    buf_ref,
    square_ref,
    flat_ref,
    gate_ref,
    *,
    images,
    length,
    experts,
    chunk,
):
    i = pl.program_id(0)
    width = x_ref.shape[2]

    @pl.when(i == 0)
    def _():
        flat_ref[...] = jnp.zeros(flat_ref.shape, F32)
        gate_ref[...] = jnp.zeros(gate_ref.shape, F32)
        square_ref[...] = jnp.zeros(square_ref.shape, F32)

    x = x_ref[0].astype(F32)
    m = col_ref[0][:, 4:5].astype(F32)
    n1, _ = ln_stats(x)
    a1 = ((n1 * gain1_ref[...] + bias1_ref[...]) * m).astype(BF)
    qkv_ref[0] = mm(a1, w_qkv_ref[...]).astype(BF)
    key_ok = row_ref[0][4:5, :] > 0
    masks = head_masks()
    lane = iota((length, PAIR), 1)
    for j in range(HEADS // 2):
        q = qkv_ref[0, :, j * PAIR : (j + 1) * PAIR]
        k = qkv_ref[0, :, width + j * PAIR : width + (j + 1) * PAIR]
        v = qkv_ref[0, :, 2 * width + j * PAIR : 2 * width + (j + 1) * PAIR]
        halves = []
        for mask in masks:
            s = mm(q * mask, k, ((1,), (1,))) * SCALE
            s = jnp.where(key_ok, s, -1e30)
            e = jnp.exp(s - jnp.max(s, axis=-1, keepdims=True))
            p = (e / jnp.sum(e, axis=-1, keepdims=True)).astype(BF)
            halves.append(mm(p, v))
        ctx_ref[0, :, j * PAIR : (j + 1) * PAIR] = jnp.where(
            lane < HEAD_DIM, halves[0], halves[1]
        ).astype(BF)
    att = mm(ctx_ref[0], w_out_ref[...]) * m
    square_ref[...] += jnp.sum(att * att, axis=0, keepdims=True)
    h = x + att
    mid_ref[0] = h
    n2, _ = ln_stats(h)
    a2 = ((n2 * gain2_ref[...] + bias2_ref[...]) * m).astype(BF)
    flat_ref[pl.ds(pl.multiple_of(i * length, 8), length), :] = a2.astype(F32)
    logits = mm(a2, w_router_ref[...])
    z = jnp.exp(logits - jnp.max(logits, axis=-1, keepdims=True))
    probs = z / jnp.sum(z, axis=-1, keepdims=True)
    expert_lane = iota((length, experts), 1)
    slot_lane = iota((length, 128), 1)
    expert_row = iota((experts, length), 0)
    for k in range(TOP):
        expert = col_ref[0][:, k : k + 1]
        slot = col_ref[0][:, TOP + k : TOP + k + 1]
        gate = jnp.sum(jnp.where(expert_lane == expert, probs, 0.0), axis=-1, keepdims=True)
        placed = jnp.where((slot_lane == slot) & (slot < CAP), gate, 0.0)
        mine = jnp.where(expert_row == row_ref[0][k : k + 1, :], 1.0, 0.0)
        gate_ref[...] += mm_exact(mine, placed)

    @pl.when(i == images - 1)
    def _():
        base = images * length
        high, mid, low = parts3(gate_ref[...])
        flat_ref[base : base + experts, 0:128] = high.astype(F32)
        flat_ref[base : base + experts, 128:256] = mid.astype(F32)
        flat_ref[base : base + experts, 256:384] = low.astype(F32)
        scatter_rows(index_ref, flat_ref, buf_ref, chunk)


def block_gates(block):
    count = block.shape[0]
    last = jnp.where(iota((count, ROWS, 1), 1) == CAP, block[:, :, 0:384].astype(F32), 0.0)
    row = jnp.sum(last, axis=1, keepdims=True)
    gates = row[:, :, 0:128] + row[:, :, 128:256] + row[:, :, 256:384]
    same = iota((count, ROWS, 128), 1) == iota((count, ROWS, 128), 2)
    return jnp.sum(jnp.where(same, gates, 0.0), axis=-1, keepdims=True)


def with_last_row(block, values):
    count, _, width = block.shape
    same = iota((count, ROWS, 128), 1) == iota((count, ROWS, 128), 2)
    row = jnp.sum(jnp.where(same, values, 0.0), axis=1, keepdims=True)
    high, mid, low = parts3(row)
    zero = jnp.zeros((count, 1, width - 384), F32)
    row = jnp.concatenate([high.astype(F32), mid.astype(F32), low.astype(F32), zero], axis=2)
    return jnp.where(iota((count, ROWS, 1), 1) == CAP, row, block).astype(BF)


def gelu_parts(pre):
    square = pre * pre
    t = jnp.tanh(CURVE * pre * (1.0 + CUBIC * square))
    half = 0.5 * (1.0 + t)
    slope = half + 0.5 * pre * (1.0 - t * t) * (CURVE * (1.0 + 3.0 * CUBIC * square))
    return pre * half, slope


def expert_kernel(
    rows_ref,
    dy_ref,
    w_in_ref,
    w_back_ref,
    grad_rows_ref,
    gated_ref,
    rows_out_ref,
    grad_out_ref,
    hidden_ref,
    grad_pre_ref,
):
    count, _, width = rows_ref.shape
    total = count * ROWS
    pieces = w_in_ref.shape[0]
    piece = w_in_ref.shape[2]
    block = rows_ref[...]
    gates = block_gates(block)
    rows = jnp.where(iota((count, ROWS, 1), 1) == CAP, 0.0, block.astype(F32)).astype(BF)
    rows = rows.reshape(total, width)
    rows_out_ref[...] = rows
    dy = dy_ref[...].astype(F32)
    grad_out = (gates * dy).astype(BF).reshape(total, width)
    grad_out_ref[...] = grad_out
    out = jnp.zeros((total, width), F32)
    grad_rows = jnp.zeros((total, width), F32)
    for q in range(pieces):
        pre = mm(rows, w_in_ref[q])
        hidden, slope = gelu_parts(pre)
        hidden = hidden.astype(BF)
        hidden_ref[:, q * piece : (q + 1) * piece] = hidden
        out = out + mm(hidden, w_back_ref[q])
        grad_pre = (mm(grad_out, w_back_ref[q], ((1,), (1,))) * slope).astype(BF)
        grad_pre_ref[:, q * piece : (q + 1) * piece] = grad_pre
        grad_rows = grad_rows + mm(grad_pre, w_in_ref[q], ((1,), (1,)))
    out = out.reshape(count, ROWS, width)
    grad_gate = jnp.sum(dy * out, axis=-1, keepdims=True)
    gated_ref[...] = (gates * out).astype(BF)
    grad_rows_ref[...] = with_last_row(grad_rows.reshape(count, ROWS, width), grad_gate)


def expert_weights_kernel(rows_ref, grad_out_ref, hidden_ref, grad_pre_ref, out_ref):
    width = rows_ref.shape[1]
    piece = hidden_ref.shape[1]
    out_ref[0, 0:width, :] = mm(rows_ref[...], grad_pre_ref[...], ((0,), (0,))).astype(BF)
    out_ref[0, width : width + piece, :] = mm(
        hidden_ref[...], grad_out_ref[...], ((0,), (0,))
    ).astype(BF)


def backward_kernel(
    back_ref,
    x_ref,
    mid_ref,
    dy_ref,
    qkv_ref,
    ctx_ref,
    col_ref,
    gain1_ref,
    bias1_ref,
    w_qkv_ref,
    w_out_ref,
    gain2_ref,
    bias2_ref,
    w_router_ref,
    grad_x_ref,
    weights_ref,
    norms_ref,
    sum_qkv_ref,
    sum_out_ref,
    sum_router_ref,
    grad_gate_ref,
    dqkv_ref,
    *,
    images,
    length,
    experts,
):
    i = pl.program_id(0)
    width = x_ref.shape[2]
    total = experts * ROWS

    @pl.when(i == 0)
    def _():
        sum_qkv_ref[...] = jnp.zeros(sum_qkv_ref.shape, F32)
        sum_out_ref[...] = jnp.zeros(sum_out_ref.shape, F32)
        sum_router_ref[...] = jnp.zeros(sum_router_ref.shape, F32)
        norms_ref[...] = jnp.zeros(norms_ref.shape, F32)
        last = iota((experts, total), 0) * ROWS + CAP == iota((experts, total), 1)
        picked = mm(jnp.where(last, 1.0, 0.0).astype(BF), back_ref[:, 0:384])
        grad_gate_ref[...] = picked[:, 0:128] + picked[:, 128:256] + picked[:, 256:384]

    col = col_ref[0]
    m = col[:, 4:5].astype(F32)
    x = x_ref[0].astype(F32)
    dy = dy_ref[0].astype(F32)
    n2, r2 = ln_stats(mid_ref[0])
    a2 = ((n2 * gain2_ref[...] + bias2_ref[...]) * m).astype(BF)
    logits = mm(a2, w_router_ref[...])
    z = jnp.exp(logits - jnp.max(logits, axis=-1, keepdims=True))
    probs = z / jnp.sum(z, axis=-1, keepdims=True)
    expert_lane = iota((length, experts), 1)
    slot_lane = iota((length, 128), 1)
    grad_probs = jnp.zeros((length, experts), F32)
    for k in range(TOP):
        slot = col[:, TOP + k : TOP + k + 1]
        mine = jnp.where(expert_lane == col[:, k : k + 1], 1.0, 0.0)
        table = mm_exact(mine, grad_gate_ref[...])
        grad_gate = jnp.sum(
            jnp.where((slot_lane == slot) & (slot < CAP), table, 0.0), axis=-1, keepdims=True
        )
        grad_probs = grad_probs + mine * grad_gate
    grad_logits = probs * (grad_probs - jnp.sum(probs * grad_probs, axis=-1, keepdims=True))
    high = grad_logits.astype(BF)
    low = (grad_logits - high.astype(F32)).astype(BF)
    sum_router_ref[...] += mm(a2, high, ((0,), (0,))) + mm(a2, low, ((0,), (0,)))
    grad_a2 = mm(one_hot_tokens(col[:, 6:8], total), back_ref[...])
    grad_a2 = grad_a2 + mm(high, w_router_ref[...], ((1,), (1,)))
    grad_a2 = grad_a2 + mm(low, w_router_ref[...], ((1,), (1,)))
    up2 = grad_a2 * m
    norms_ref[2:3, :] += jnp.sum(up2 * n2, axis=0, keepdims=True)
    norms_ref[3:4, :] += jnp.sum(up2, axis=0, keepdims=True)
    grad_mid = dy + ln_back(up2, n2, r2, gain2_ref[...])
    grad_att = (grad_mid * m).astype(BF)
    sum_out_ref[...] += mm(ctx_ref[0], grad_att, ((0,), (0,)))
    grad_ctx = mm(grad_att, w_out_ref[...], ((1,), (1,))).astype(BF)
    masks = head_masks()
    for j in range(HEADS // 2):
        q = qkv_ref[0, :, j * PAIR : (j + 1) * PAIR]
        k = qkv_ref[0, :, width + j * PAIR : width + (j + 1) * PAIR]
        v = qkv_ref[0, :, 2 * width + j * PAIR : 2 * width + (j + 1) * PAIR]
        g = grad_ctx[:, j * PAIR : (j + 1) * PAIR]
        dq = jnp.zeros((length, PAIR), F32)
        dk = jnp.zeros((length, PAIR), F32)
        dv = jnp.zeros((length, PAIR), F32)
        for mask in masks:
            qm = q * mask
            gm = g * mask
            s = mm(k, qm, ((1,), (1,))) * SCALE
            s = jnp.where(m > 0, s, -1e30)
            e = jnp.exp(s - jnp.max(s, axis=0, keepdims=True))
            p = e / jnp.sum(e, axis=0, keepdims=True)
            dp = mm(v, gm, ((1,), (1,)))
            ds = (p * (dp - jnp.sum(p * dp, axis=0, keepdims=True))).astype(BF)
            dv = dv + mm(p.astype(BF), gm)
            dk = dk + mm(ds, qm)
            dq = dq + mm(ds, k * mask, ((0,), (0,)))
        dqkv_ref[:, j * PAIR : (j + 1) * PAIR] = (dq * SCALE).astype(BF)
        dqkv_ref[:, width + j * PAIR : width + (j + 1) * PAIR] = (dk * SCALE).astype(BF)
        dqkv_ref[:, 2 * width + j * PAIR : 2 * width + (j + 1) * PAIR] = dv.astype(BF)
    n1, r1 = ln_stats(x)
    a1 = ((n1 * gain1_ref[...] + bias1_ref[...]) * m).astype(BF)
    dqkv = dqkv_ref[...]
    sum_qkv_ref[...] += mm(a1, dqkv, ((0,), (0,)))
    up1 = mm(dqkv, w_qkv_ref[...], ((1,), (1,))) * m
    norms_ref[0:1, :] += jnp.sum(up1 * n1, axis=0, keepdims=True)
    norms_ref[1:2, :] += jnp.sum(up1, axis=0, keepdims=True)
    grad_x_ref[0] = (grad_mid + ln_back(up1, n1, r1, gain1_ref[...])).astype(BF)

    @pl.when(i == images - 1)
    def _():
        weights_ref[:, 0 : 3 * width] = sum_qkv_ref[...].astype(BF)
        weights_ref[:, 3 * width : 4 * width] = sum_out_ref[...].astype(BF)
        weights_ref[:, 4 * width : 4 * width + experts] = sum_router_ref[...].astype(BF)


def final_kernel(back_ref, mid_ref, col_ref, out_ref, squares_ref):
    i = pl.program_id(0)

    @pl.when(i == 0)
    def _():
        squares_ref[...] = jnp.zeros(squares_ref.shape, F32)

    col = col_ref[0]
    m = col[:, 4:5].astype(F32)
    moe = mm(one_hot_tokens(col[:, 6:8], back_ref.shape[0]), back_ref[...])
    y = mid_ref[0] + moe
    out_ref[0] = y.astype(BF)
    squares_ref[0:1, :] += jnp.sum(moe * moe, axis=0, keepdims=True)
    squares_ref[1:2, :] += jnp.sum(m * y * y, axis=0, keepdims=True)


def whole(array):
    zeros = (0,) * array.ndim
    return pl.BlockSpec(array.shape, lambda *_: zeros)


def whole_out(shape):
    zeros = (0,) * len(shape)
    return pl.BlockSpec(shape, lambda *_: zeros)


def per_image(array):
    rest = array.shape[1:]
    zeros = (0,) * len(rest)
    return pl.BlockSpec((1,) + rest, lambda i: (i,) + zeros)


PARAMS = pltpu.CompilerParams(vmem_limit_bytes=VMEM)


def exchange(v, axes):
    return lax.all_to_all(v, axes, split_axis=0, concat_axis=0, tiled=True)


def experts_here(rows, dy_rows, w_in_all, w_back_all):
    w_in, w_back = w_in_all, w_back_all
    devices, _, width = rows.shape
    pieces, _, piece = w_in.shape
    step = 8 if devices % 8 == 0 else 1
    total = devices * ROWS
    block3 = pl.BlockSpec((step, ROWS, width), lambda i: (i, 0, 0))
    block2 = pl.BlockSpec((step * ROWS, width), lambda i: (i, 0))
    wide2 = pl.BlockSpec((step * ROWS, pieces * piece), lambda i: (i, 0))
    grad_rows, gated, rows_low, grad_out, hidden, grad_pre = pl.pallas_call(
        expert_kernel,
        grid=(devices // step,),
        in_specs=[block3, block3, whole(w_in), whole(w_back)],
        out_specs=[block3, block3, block2, block2, wide2, wide2],
        out_shape=[
            jax.ShapeDtypeStruct((devices, ROWS, width), BF),
            jax.ShapeDtypeStruct((devices, ROWS, width), BF),
            jax.ShapeDtypeStruct((total, width), BF),
            jax.ShapeDtypeStruct((total, width), BF),
            jax.ShapeDtypeStruct((total, pieces * piece), BF),
            jax.ShapeDtypeStruct((total, pieces * piece), BF),
        ],
        compiler_params=PARAMS,
        name="experts",
    )(rows, dy_rows, w_in, w_back)
    column = pl.BlockSpec((total, piece), lambda q: (0, q))
    grads = pl.pallas_call(
        expert_weights_kernel,
        grid=(pieces,),
        in_specs=[whole(rows_low), whole(grad_out), column, column],
        out_specs=pl.BlockSpec((1, width + piece, width), lambda q: (q, 0, 0)),
        out_shape=jax.ShapeDtypeStruct((pieces, width + piece, width), BF),
        compiler_params=PARAMS,
        name="expert_weights",
    )(rows_low, grad_out, hidden, grad_pre)
    return grad_rows, gated, grads


def experts_split(rows, dy_rows, w_in, w_back, groups):
    local, width, _ = w_in.shape
    block = rows.reshape(groups * local, ROWS, width)
    last = block[:, CAP, :384].astype(F32).reshape(-1, 3, 128).sum(axis=1)
    gates = last[:, :ROWS, None]
    rows = block.at[:, CAP].set(0).reshape(groups, local, ROWS, width)
    dy = dy_rows.reshape(groups * local, ROWS, width).astype(F32)
    grad_out = (gates * dy).astype(BF).reshape(groups, local, ROWS, width)
    rows_all = lax.all_gather(rows, "weight", axis=0, tiled=True)
    grad_all = lax.all_gather(grad_out, "weight", axis=0, tiled=True)
    pre = jnp.einsum("gecd,edf->gecf", rows_all, w_in, preferred_element_type=F32)
    hidden, slope = gelu_parts(pre)
    hidden = hidden.astype(BF)
    out = jnp.einsum("gecf,efd->gecd", hidden, w_back, preferred_element_type=F32)
    out = lax.psum_scatter(out.astype(BF), "weight", scatter_dimension=0, tiled=True)
    out = out.astype(F32).reshape(groups * local, ROWS, width)
    grad_hidden = jnp.einsum("gecd,efd->gecf", grad_all, w_back, preferred_element_type=F32)
    grad_pre = (grad_hidden * slope).astype(BF)
    grad_rows = jnp.einsum("gecf,edf->gecd", grad_pre, w_in, preferred_element_type=F32)
    grad_rows = lax.psum_scatter(
        grad_rows.astype(BF), "weight", scatter_dimension=0, tiled=True
    ).reshape(groups * local, ROWS, width)
    grad_in = jnp.einsum("gecd,gecf->edf", rows_all, grad_pre, preferred_element_type=F32)
    grad_back = jnp.einsum("gecf,gecd->efd", hidden, grad_all, preferred_element_type=F32)
    gated = (gates * out).astype(BF)
    row = jnp.pad(jnp.sum(dy * out, axis=-1), ((0, 0), (0, 128 - ROWS)))
    row = jnp.concatenate(list(parts3(row)), axis=1)
    grad_rows = grad_rows.at[:, CAP, :384].set(row)
    shape = (groups, local * ROWS, width)
    return grad_rows.reshape(shape), gated.reshape(shape), grad_in, grad_back


def on_device(
    tokens,
    valid,
    experts,
    slots,
    ln1_gain,
    ln1_bias,
    w_qkv,
    w_out,
    ln2_gain,
    ln2_bias,
    w_router,
    w_in,
    w_back,
    cotangent,
):
    images, length, width = tokens.shape
    token_count = images * length
    expert_count = w_in.shape[0]
    groups = lax.axis_size("dp") * lax.axis_size("seq")
    members = lax.axis_size("weight")
    devices = groups * members
    local = expert_count // groups
    alone = local == members
    first = (lax.axis_index("dp") * lax.axis_size("seq") + lax.axis_index("seq")) * local
    w_in_mine = lax.dynamic_slice_in_dim(w_in, first, local, 0)
    w_back_mine = lax.dynamic_slice_in_dim(w_back, first, local, 0)
    if alone:
        w_in_mine = exchange(w_in_mine, "weight")
        w_back_mine = exchange(w_back_mine, "weight")

    kept = slots < CAP
    flat = jnp.where(kept, experts * ROWS + slots, -1)
    col = jnp.concatenate(
        [experts, slots, valid[:, :, None], jnp.zeros_like(valid)[:, :, None], flat], axis=2
    )
    row = jnp.swapaxes(col, 1, 2)
    padded = -(-(token_count + expert_count) // 128) * 128
    spare = jnp.arange(expert_count, dtype=jnp.int32) * ROWS + CAP
    index = jnp.concatenate(
        [
            flat.reshape(token_count, TOP).T,
            jnp.stack([spare, jnp.full_like(spare, -1)]),
            jnp.full((TOP, padded - token_count - expert_count), -1, jnp.int32),
        ],
        axis=1,
    )
    gain1, bias1, gain2, bias2 = (
        v.reshape(1, width) for v in (ln1_gain, ln1_bias, ln2_gain, ln2_bias)
    )
    chunk = 8 if expert_count % 8 == 0 else 1
    buffer_shape = jax.ShapeDtypeStruct((expert_count, ROWS, width), BF)
    flat_scratch = pltpu.VMEM((padded, width), F32)

    dy_rows = pl.pallas_call(
        functools.partial(send_kernel, images=images, length=length, chunk=chunk),
        out_shape=buffer_shape,
        scratch_shapes=[flat_scratch],
        compiler_params=PARAMS,
        name="send_dy",
    )(index, cotangent)

    rows_shape = (devices, ROWS, width) if alone else (groups, local * ROWS, width)
    route = EVERY if alone else GROUP
    dy_rows = exchange(dy_rows.reshape(rows_shape), route)

    qkv, ctx, mid, rows, att_squares = pl.pallas_call(
        functools.partial(
            forward_kernel, images=images, length=length, experts=expert_count, chunk=chunk
        ),
        grid=(images,),
        in_specs=[
            per_image(tokens),
            per_image(col),
            per_image(row),
            whole(index),
            whole(gain1),
            whole(bias1),
            whole(w_qkv),
            whole(w_out),
            whole(gain2),
            whole(bias2),
            whole(w_router),
        ],
        out_specs=[
            pl.BlockSpec((1, length, 3 * width), lambda i: (i, 0, 0)),
            pl.BlockSpec((1, length, width), lambda i: (i, 0, 0)),
            pl.BlockSpec((1, length, width), lambda i: (i, 0, 0)),
            whole_out((expert_count, ROWS, width)),
            whole_out((1, width)),
        ],
        out_shape=[
            jax.ShapeDtypeStruct((images, length, 3 * width), BF),
            jax.ShapeDtypeStruct((images, length, width), BF),
            jax.ShapeDtypeStruct((images, length, width), F32),
            buffer_shape,
            jax.ShapeDtypeStruct((1, width), F32),
        ],
        scratch_shapes=[flat_scratch, pltpu.VMEM((expert_count, 128), F32)],
        compiler_params=PARAMS,
        name="forward",
    )(tokens, col, row, index, gain1, bias1, w_qkv, w_out, gain2, bias2, w_router)

    rows = exchange(rows.reshape(rows_shape), route)
    if alone:
        grad_rows, gated, grads = experts_here(rows, dy_rows, w_in_mine, w_back_mine)
    else:
        grad_rows, gated, grad_in, grad_back = experts_split(
            rows, dy_rows, w_in_mine, w_back_mine, groups
        )
    back_shape = (expert_count * ROWS, width)
    grad_rows = exchange(grad_rows, route).reshape(back_shape)
    gated = exchange(gated, route).reshape(back_shape)
    if alone:
        grads = exchange(grads, "weight").astype(F32)
        grad_in = grads[:, :width]
        grad_back = grads[:, width:]

    packed = 4 * width + -(-expert_count // 128) * 128
    grad_tokens, weight_sums, norm_sums = pl.pallas_call(
        functools.partial(backward_kernel, images=images, length=length, experts=expert_count),
        grid=(images,),
        in_specs=[
            whole(grad_rows),
            per_image(tokens),
            per_image(mid),
            per_image(cotangent),
            per_image(qkv),
            per_image(ctx),
            per_image(col),
            whole(gain1),
            whole(bias1),
            whole(w_qkv),
            whole(w_out),
            whole(gain2),
            whole(bias2),
            whole(w_router),
        ],
        out_specs=[
            pl.BlockSpec((1, length, width), lambda i: (i, 0, 0)),
            whole_out((width, packed)),
            whole_out((4, width)),
        ],
        out_shape=[
            jax.ShapeDtypeStruct((images, length, width), BF),
            jax.ShapeDtypeStruct((width, packed), BF),
            jax.ShapeDtypeStruct((4, width), F32),
        ],
        scratch_shapes=[
            pltpu.VMEM((width, 3 * width), F32),
            pltpu.VMEM((width, width), F32),
            pltpu.VMEM((width, expert_count), F32),
            pltpu.VMEM((expert_count, 128), F32),
            pltpu.VMEM((length, 3 * width), BF),
        ],
        compiler_params=PARAMS,
        name="backward",
    )(
        grad_rows,
        tokens,
        mid,
        cotangent,
        qkv,
        ctx,
        col,
        gain1,
        bias1,
        w_qkv,
        w_out,
        gain2,
        bias2,
        w_router,
    )

    output, moe_squares = pl.pallas_call(
        final_kernel,
        grid=(images,),
        in_specs=[whole(gated), per_image(mid), per_image(col)],
        out_specs=[
            pl.BlockSpec((1, length, width), lambda i: (i, 0, 0)),
            whole_out((2, width)),
        ],
        out_shape=[
            jax.ShapeDtypeStruct((images, length, width), BF),
            jax.ShapeDtypeStruct((2, width), F32),
        ],
        compiler_params=PARAMS,
        name="final",
    )(gated, mid, col)

    plane = lax.axis_size("dp") * members
    depth = lax.axis_size("seq")
    share = width // plane
    total = exchange(weight_sums.reshape(plane, share, packed), PLANE)
    total = jnp.sum(total.astype(F32), axis=0).astype(BF)
    total = exchange(total.reshape(depth, share // depth, packed), "seq")
    total = jnp.sum(total.astype(F32), axis=0).astype(BF)
    total = exchange(jnp.broadcast_to(total[None], (depth,) + total.shape), "seq")
    total = total.reshape(share, packed)
    total = exchange(jnp.broadcast_to(total[None], (plane,) + total.shape), PLANE)
    total = total.reshape(width, packed).astype(F32)

    small = jnp.concatenate(
        [norm_sums, att_squares, moe_squares, jnp.zeros((1, width), F32)], axis=0
    )
    small = exchange(jnp.broadcast_to(small[None], (devices,) + small.shape), EVERY)
    small = jnp.sum(small, axis=0)
    rms_values = jnp.sqrt(
        jnp.sum(small[4:7], axis=1) / float(images * devices * VALID * width)
    )
    return (
        output,
        grad_tokens,
        small[0],
        small[1],
        total[:, : 3 * width],
        total[:, 3 * width : 4 * width],
        small[2],
        small[3],
        total[:, 4 * width : 4 * width + expert_count],
        grad_in,
        grad_back,
        rms_values,
    )


def solution(mesh):
    spread = P(("dp", "seq", "weight"), None, None)
    placed = (
        spread,
        P(("dp", "seq", "weight"), None),
        spread,
        spread,
        P(),
        P(),
        P(),
        P(),
        P(),
        P(),
        P(),
        P(None, None, "weight"),
        P(None, "weight", None),
        spread,
    )
    return jax.shard_map(
        on_device,
        mesh=mesh,
        in_specs=placed,
        out_specs=(
            spread,
            spread,
            P(),
            P(),
            P(),
            P(),
            P(),
            P(),
            P(),
            P(("dp", "seq"), None, "weight"),
            P(("dp", "seq"), "weight", None),
            P(),
        ),
        check_vma=False,
    )
```
